256 devices in a mesh: dp: 32 (over x, z), block: 8 (over y, core).
Axes of the slice: x: 4, y: 4, z: 8, core: 2. Of those that a mesh axis runs over, the one named last changes fastest.
Arguments:
- tokens: bfloat16 [32, 256, 4096], P('dp', 'block'), may hold values from -6 to 6
- cotangent: bfloat16 [32, 256, 4096], P('dp', 'block'), may hold values from -6 to 6
- w_up: bfloat16 [8, 4096, 512], P('block'), may hold values from -0.09375 to 0.09375
- w_down: bfloat16 [8, 512, 4096], P('block'), may hold values from -0.25 to 0.25
- active: int32 [32, 8], replicated, may hold values from 0 to 1, as said below
- width: int32 [32], replicated, may hold values from 8 to 16
- counts: int32 [8], replicated, may hold values from 32 to 127
Outputs:
- mixed: bfloat16 [32, 256, 4096], P('dp', 'block')
- input_grad: bfloat16 [32, 256, 4096], P('dp', 'block')
- up_grad: float32 [8, 4096, 512], P('block', 'dp')
- down_grad: float32 [8, 512, 4096], P('block', None, 'dp')
The draws below stay inside these ranges and needn't reach their ends.
Inputs may be any that keep to these rules, and one draw needn't show every extreme that they name: `active`: 0 or 1; blocks differ in how many micro-batches use them. micro-batch i uses the first 256 * width[i] features.
All inputs are finite; a program needn't handle non-finite values.
Results may differ from the reference program's by a relative error of at most 0.019.
Values may be sent and summed in bfloat16 or wider, within the bound.
No kernel may reach another device: no remote copies, remote signals or barrier semaphores. Data moves between devices by JAX's collectives and lax.ppermute only.
A program may use at most 128 MiB of HBM per device.

```python
import math
import jax
import jax.numpy as jnp
from jax import lax

D = 4096
UNITS = 512
BLK_DEV = 1
MB_ROWS = 256
NBLK = 8
NMB = 32
WSTEP = 256
N_DP = 32
N_BLOCK = 8


def draw_active(key, part):
    key_rates, key_values = jax.random.split(jax.random.fold_in(key, 7))
    use_rates = jax.random.randint(key_rates, (NBLK,), 1, 8)
    raw_draws = jax.random.randint(key_values, (NMB, NBLK), 0, 8)
    return (raw_draws < use_rates[None, :]).astype(jnp.int32)


def touch_ends(result, rng, low, high):
    dims = result.shape
    index_at = [jax.random.randint(jax.random.fold_in(rng, axis), (), 0, dims[axis]) for axis in range(len(dims))]
    result = result.at[tuple(index_at)].set(low)
    longest = dims.index(max(dims))
    index_at[longest] = (index_at[longest] + 1) % dims[longest]
    return result.at[tuple(index_at)].set(high)


def with_spikes(result, key, source, target, parts, factor):
    owner, partner = [(jnp.arange(result.shape[position]) // (result.shape[position] // parts)).reshape([-1 if axis == position else 1 for axis in range(result.ndim)]) for position in (source, target)]
    chosen = jax.random.permutation(key, parts)[partner]
    strong = (owner == chosen) | (owner == (partner + parts // 2) % parts)
    return jnp.where(strong, factor * result, result)


def block_scale(key, extent, cuts, low, largest):
    level = 1.0
    for position, blocks in cuts:
        draws = jax.random.uniform(jax.random.fold_in(jax.random.fold_in(key, 6), position), (blocks,), jnp.float32, low / len(cuts), largest / len(cuts))
        level = level * jnp.repeat(jnp.exp(draws), extent[position] // blocks).reshape((-1,) + (1,) * (len(extent) - 1 - position))
    return level


def centred(rng, extent, scale, reach, cuts=(), kind=jnp.bfloat16):
    drawn = jax.random.normal(rng, extent, jnp.float32) * scale
    if len(cuts) > 0:
        drawn = block_scale(rng, extent, cuts, -0.22, 0.18) * drawn
    return jnp.clip(drawn, min=-reach, max=reach).astype(kind)


def heavy_noise(own_key, dims, scale, bound, pieces, heavy, held_as=jnp.bfloat16):
    result = scale * jax.random.normal(own_key, dims, jnp.float32)
    if pieces:
        result = result * block_scale(own_key, dims, pieces, -0.22, 0.18)
    return jnp.clip(with_spikes(result, jax.random.fold_in(own_key, 3), *heavy), -bound, bound).astype(held_as)


def setup_inputs(seed: int = 0) -> dict:
    streams_of = jax.random.split(jax.random.key(seed), 8)
    tokens = heavy_noise(streams_of[0], (NMB, MB_ROWS, D), 1.0, 6.0, ((0, 32), (1, 8)), (0, 2, 32, 2.75))
    cotangent = centred(streams_of[1], (NMB, MB_ROWS, D), 1.0, 6.0, ((0, 32), (1, 8)))
    w_up = centred(streams_of[2], (NBLK, D, UNITS), D ** -0.5, 0.09375, ((0, 8),))
    w_down = centred(streams_of[3], (NBLK, UNITS, D), UNITS ** -0.5, 0.25, ((0, 8),))
    active = draw_active(jax.random.fold_in(streams_of[7], 71), 0)
    width = touch_ends(jax.random.randint(streams_of[5], (NMB,), 8, 17), jax.random.fold_in(streams_of[5], 1), 8, 16).astype(jnp.int32)
    counts = touch_ends(jax.random.randint(streams_of[6], (NBLK,), N_DP, 4 * N_DP), jax.random.fold_in(streams_of[6], 1), N_DP, (4 * N_DP) - 1).astype(jnp.int32)
    return dict(tokens=tokens, cotangent=cotangent, w_up=w_up, w_down=w_down, active=active, width=width, counts=counts)


GELU_C = math.sqrt(2.0 / math.pi)

def gelu_parts(pre_vals):
    tanh_val = jnp.tanh(GELU_C * (pre_vals + 0.044715 * pre_vals * pre_vals * pre_vals))
    gelu_value = 0.5 * pre_vals * (1.0 + tanh_val)
    gelu_slope = 0.5 * (1.0 + tanh_val) + 0.5 * pre_vals * (1.0 - tanh_val * tanh_val) * GELU_C * (1.0 + 3.0 * 0.044715 * pre_vals * pre_vals)
    return (gelu_value, gelu_slope)

def round_trip(values):
    return lax.optimization_barrier(values.astype(jnp.bfloat16)).astype(jnp.float32)

def group_round(terms):
    grouped = terms.reshape(N_BLOCK, BLK_DEV, MB_ROWS, D).sum(axis=1)
    return round_trip(grouped).sum(axis=0)

def reference(tokens, cotangent, w_up, w_down, active, width, counts):
    up_full = w_up.astype(jnp.float32)
    down_full = w_down.astype(jnp.float32)
    gate_all = active.astype(jnp.float32)
    scale_all = gate_all / counts.astype(jnp.float32)[None, :]
    feat_ids = jnp.arange(D, dtype=jnp.int32)

    def one_batch(carry, inputs):
        up_acc, down_acc = carry
        x_rows, dy_rows, gate_row, scale_row, width_step = inputs
        feat_mask = (feat_ids < WSTEP * width_step).astype(jnp.bfloat16)
        masked_x = x_rows * feat_mask
        masked_dy = dy_rows * feat_mask
        pre_act = jnp.einsum('rd,bdu->bru', masked_x.astype(jnp.float32), up_full)
        gelu_value, gelu_slope = gelu_parts(pre_act)
        hidden = gelu_value.astype(jnp.bfloat16)
        out_terms = jnp.einsum('bru,bud->brd', hidden.astype(jnp.float32), down_full) * gate_row[:, None, None]
        mixed = (x_rows.astype(jnp.float32) + feat_mask.astype(jnp.float32) * group_round(out_terms)).astype(jnp.bfloat16)
        back_proj = jnp.einsum('rd,bud->bru', masked_dy.astype(jnp.float32), down_full)
        grad_hidden = (back_proj * gelu_slope).astype(jnp.bfloat16)
        in_terms = jnp.einsum('bru,bdu->brd', grad_hidden.astype(jnp.float32), up_full) * gate_row[:, None, None]
        input_grad = (dy_rows.astype(jnp.float32) + feat_mask.astype(jnp.float32) * group_round(in_terms)).astype(jnp.bfloat16)
        down_term = round_trip(scale_row[:, None, None] * jnp.einsum('bru,rd->bud', hidden.astype(jnp.float32), masked_dy.astype(jnp.float32)))
        up_term = round_trip(scale_row[:, None, None] * jnp.einsum('rd,bru->bdu', masked_x.astype(jnp.float32), grad_hidden.astype(jnp.float32)))
        return ((up_acc + up_term, down_acc + down_term), (mixed, input_grad))
    init = (jnp.zeros((NBLK, D, UNITS), jnp.float32), jnp.zeros((NBLK, UNITS, D), jnp.float32))
    sums, rows_out = lax.scan(one_batch, init, (tokens, cotangent, gate_all, scale_all, width))
    return (rows_out[0], rows_out[1], sums[0], sums[1])
```

```python
import math

import jax
import jax.numpy as jnp
from jax import lax
from jax.sharding import PartitionSpec as P

GELU_C = math.sqrt(2.0 / math.pi)
NX, NZ, NY, NC = 4, 8, 4, 2
BF = jnp.bfloat16
F32 = jnp.float32


def gelu_parts(pre_vals):
    tanh_val = jnp.tanh(GELU_C * (pre_vals + 0.044715 * pre_vals * pre_vals * pre_vals))
    gelu_value = 0.5 * pre_vals * (1.0 + tanh_val)
    gelu_slope = 0.5 * (1.0 + tanh_val) + 0.5 * pre_vals * (1.0 - tanh_val * tanh_val) * GELU_C * (
        1.0 + 3.0 * 0.044715 * pre_vals * pre_vals
    )
    return (gelu_value, gelu_slope)


def to_y(v, k):
    return lax.ppermute(v, "block", [(i, (i + 2 * k) % 8) for i in range(8)])


def to_core(v):
    return lax.ppermute(v, "block", [(i, i ^ 1) for i in range(8)])


def to_x(v, k):
    return lax.ppermute(v, "dp", [(i, ((i // NZ + k) % NX) * NZ + i % NZ) for i in range(NX * NZ)])


def to_z(v, k):
    return lax.ppermute(v, "dp", [(i, (i // NZ) * NZ + (i % NZ + k) % NZ) for i in range(NX * NZ)])


def ring_gather(v, send):
    half = v.shape[0] // 2
    before = send(v, 1)
    after = send(v, -1)
    far = jnp.concatenate([send(before[:half], 1), send(after[half:], -1)], axis=0)
    return [v, after, far, before]


def gather_block(v):
    mine = jnp.concatenate(ring_gather(v, to_y), axis=0)
    return jnp.concatenate([mine, to_core(mine)], axis=0)


def scatter_block(parts):
    rows = parts.shape[0] // 8
    mine, other = parts[: 4 * rows], parts[4 * rows :].astype(BF)
    mine = mine + to_core(other).astype(F32)
    own, after, far, before = (mine[k * rows : (k + 1) * rows] for k in range(4))
    half = rows // 2
    low = to_y(far[:half].astype(BF), 1).astype(F32)
    high = to_y(far[half:].astype(BF), -1).astype(F32)
    after = jnp.concatenate([after[:half] + low, after[half:]], axis=0)
    before = jnp.concatenate([before[:half], before[half:] + high], axis=0)
    return own + to_y(after.astype(BF), 1).astype(F32) + to_y(before.astype(BF), -1).astype(F32)


def scatter_z(terms, z):
    half = terms.shape[1] // 2
    pick = lambda k: lax.dynamic_index_in_dim(terms, (z + k) % NZ, 0, keepdims=False)
    far = pick(4)
    low = to_z(far[:half].astype(BF), 1).astype(F32)
    high = to_z(far[half:].astype(BF), -1).astype(F32)
    up, down = pick(3), pick(-3)
    up = jnp.concatenate([up[:half] + low, up[half:]], axis=0)
    down = jnp.concatenate([down[:half], down[half:] + high], axis=0)
    for k in (2, 1):
        up = pick(k) + to_z(up.astype(BF), 1).astype(F32)
        down = pick(-k) + to_z(down.astype(BF), -1).astype(F32)
    return pick(0) + to_z(up.astype(BF), 1).astype(F32) + to_z(down.astype(BF), -1).astype(F32)


def dot(a, b, ca, cb):
    return lax.dot_general(a, b, (((ca,), (cb,)), ((), ())), preferred_element_type=F32)


def local(tokens, cotangent, w_up, w_down, active, width, counts):
    dp = lax.axis_index("dp")
    blk = lax.axis_index("block")
    x, z = dp // NZ, dp % NZ
    feats = tokens.shape[2]
    gate = lax.dynamic_slice(active, (dp, blk), (1, 1))[0, 0].astype(F32)
    count = lax.dynamic_slice(counts, (blk,), (1,))[0].astype(F32)
    limit = feats // 16 * lax.dynamic_slice(width, (dp,), (1,))[0]
    mask = (lax.iota(jnp.int32, feats) < limit).astype(BF)
    w1, w2 = w_up[0], w_down[0]
    my_x, my_dy = tokens[0] * mask, cotangent[0] * mask

    all_x = gather_block(my_x)
    all_dy = gather_block(my_dy)

    quarter = feats // NX

    def for_x(v, k):
        return lax.dynamic_slice(v, (0, ((x + k) % NX) * quarter), (v.shape[0], quarter))

    swapped = [
        to_x(jnp.concatenate([for_x(my_x, k), for_x(my_dy, k)], axis=1), k) for k in (-1, 2, 1)
    ]
    extra = gather_block(jnp.concatenate(swapped, axis=1))

    pre = dot(all_x, w1, 1, 0)
    gelu_value, gelu_slope = gelu_parts(pre)
    hidden = (gelu_value * gate).astype(BF)
    back = dot(all_dy, w2, 1, 1)
    grad_hidden = (back * (gelu_slope * gate)).astype(BF)

    mixed_sum = scatter_block(dot(hidden, w2, 1, 0))
    input_sum = scatter_block(dot(grad_hidden, w1, 1, 1))

    def terms(mine, which, h):
        others = [extra[:, (2 * k + which) * quarter :][:, :quarter] for k in range(3)]
        left = jnp.concatenate([for_x(mine, 0)] + others, axis=0)
        right = jnp.concatenate(ring_gather(h, to_x), axis=0)
        return dot(left, right, 0, 0).reshape(NZ, quarter // NZ, -1)

    scale = 1.0 / count
    down_grad = scatter_z(terms(all_dy, 1, hidden), z).T * scale
    up_grad = scatter_z(terms(all_x, 0, grad_hidden), z) * scale

    mask_float = mask.astype(F32)
    mixed = (tokens[0].astype(F32) + mask_float * mixed_sum).astype(BF)[None]
    input_grad = (cotangent[0].astype(F32) + mask_float * input_sum).astype(BF)[None]
    return (mixed, input_grad, up_grad[None], down_grad[None])


def solution(mesh):
    in_specs = (
        P("dp", "block", None),
        P("dp", "block", None),
        P("block", None, None),
        P("block", None, None),
        P(),
        P(),
        P(),
    )
    out_specs = (
        P("dp", "block", None),
        P("dp", "block", None),
        P("block", "dp", None),
        P("block", None, "dp"),
    )
    return jax.shard_map(local, mesh=mesh, in_specs=in_specs, out_specs=out_specs, check_vma=False)
```

```python
import math

import jax
import jax.numpy as jnp
from jax import lax
from jax.experimental import pallas as pl
from jax.experimental.pallas import tpu as pltpu
from jax.sharding import PartitionSpec as P

GELU_C = math.sqrt(2.0 / math.pi)
NX, NZ, NY, NC = 4, 8, 4, 2
BF = jnp.bfloat16
F32 = jnp.float32


def gelu_parts(pre_vals):
    tanh_val = jnp.tanh(GELU_C * (pre_vals + 0.044715 * pre_vals * pre_vals * pre_vals))
    gelu_value = 0.5 * pre_vals * (1.0 + tanh_val)
    gelu_slope = 0.5 * (1.0 + tanh_val) + 0.5 * pre_vals * (1.0 - tanh_val * tanh_val) * GELU_C * (
        1.0 + 3.0 * 0.044715 * pre_vals * pre_vals
    )
    return (gelu_value, gelu_slope)


def to_y(v, k):
    return lax.ppermute(v, "block", [(i, (i + 2 * k) % 8) for i in range(8)])


def to_core(v):
    return lax.ppermute(v, "block", [(i, i ^ 1) for i in range(8)])


def to_x(v, k):
    return lax.ppermute(v, "dp", [(i, ((i // NZ + k) % NX) * NZ + i % NZ) for i in range(NX * NZ)])


def to_z(v, k):
    return lax.ppermute(v, "dp", [(i, (i // NZ) * NZ + (i % NZ + k) % NZ) for i in range(NX * NZ)])


VM = pl.BlockSpec(memory_space=pltpu.VMEM)
SM = pl.BlockSpec(memory_space=pltpu.SMEM)
WSTEP = 256
ORDER = (0, -1, 2, 1)


def call(kernel, ins, outs, flops, moved, scratch=()):
    return pl.pallas_call(
        kernel,
        out_shape=[jax.ShapeDtypeStruct(shape, kind) for shape, kind in outs],
        in_specs=[spec for _, spec in ins],
        out_specs=[VM for _ in outs],
        scratch_shapes=list(scratch),
        compiler_params=pltpu.CompilerParams(vmem_limit_bytes=24 * 1024 * 1024),
        cost_estimate=pl.CostEstimate(flops=1, bytes_accessed=1, transcendentals=0),
    )(*[v for v, _ in ins])


def near(send, v, after=(None, None, None)):
    return [send(then(v, a), k) for k, a in zip((1, 2, -1), after)]


def then(v, after):
    return v if after is None else lax.optimization_barrier((v, after))[0]


def swap_y(v):
    groups = [[2 * y + c for y in range(NY)] for c in range(NC)]
    return lax.all_to_all(v, "block", 0, 0, tiled=True, axis_index_groups=groups)


def dot(a, b, ca, cb):
    return lax.dot_general(a, b, (((ca,), (cb,)), ((), ())), preferred_element_type=F32)


def live(width, at, n, kind):
    limit = WSTEP * width[lax.axis_index("dp")]
    return (at + lax.broadcasted_iota(jnp.int32, (1, n), 1) < limit).astype(F32).astype(kind)


def quarter_kernel(x_ref, dy_ref, width, *outs):
    quarter = x_ref.shape[2] // NX
    x = lax.axis_index("dp") // NZ
    for out, k in zip(outs, (1, 2, -1)):
        at = pl.multiple_of(lax.rem(x + k + NX, NX) * quarter, quarter)
        mask = live(width, at, quarter, BF)
        out[:, :quarter] = x_ref[0, :, pl.ds(at, quarter)] * mask
        out[:, quarter:] = dy_ref[0, :, pl.ds(at, quarter)] * mask


def masked_rows(mine, other, width, at, n):
    at = pl.multiple_of(at, n)
    rows = jnp.concatenate([mine[:, pl.ds(at, n)], other[:, pl.ds(at, n)]], axis=0)
    return rows * live(width, at, n, BF)


def hidden_kernel(mine, other, w1, width, active, hidden, slope, acc):
    n = 1024
    acc[...] = jnp.zeros_like(acc)

    @pl.loop(0, mine.shape[1] // n)
    def _(j):
        at = pl.multiple_of(j * n, n)
        acc[...] += dot(masked_rows(mine, other, width, at, n), w1[0, pl.ds(at, n), :], 1, 0)

    gate = active[lax.axis_index("dp"), lax.axis_index("block")].astype(F32)
    rows = 32

    @pl.loop(0, acc.shape[0] // rows)
    def _(j):
        at = pl.ds(pl.multiple_of(j * rows, rows), rows)
        value, grad = gelu_parts(acc[at, :])
        hidden[at, :] = (value * gate).astype(BF)
        slope[at, :] = grad * gate


def grad_kernel(mine, other, w2, width, slope, grad, acc):
    n = 1024
    acc[...] = jnp.zeros_like(acc)

    @pl.loop(0, mine.shape[1] // n)
    def _(j):
        at = pl.multiple_of(j * n, n)
        acc[...] += dot(masked_rows(mine, other, width, at, n), w2[0, :, pl.ds(at, n)], 1, 1)

    grad[...] = (acc[...] * slope[...]).astype(BF)


def parts_of(rows, hidden, grad, w1, w2, width, at, n):
    mask = live(width, at, n, F32)
    out = dot(hidden[rows, :], w2[0, :, pl.ds(at, n)], 1, 0) * mask
    back = dot(grad[rows, :], w1[0, pl.ds(at, n), :], 1, 1) * mask
    return out, back


def other_kernel(hidden, grad, w1, w2, width, out):
    n, feats = 512, w1.shape[1]
    half = hidden.shape[0] // 2

    @pl.loop(0, feats // n)
    def _(j):
        at = pl.multiple_of(j * n, n)
        a, b = parts_of(pl.ds(half, half), hidden, grad, w1, w2, width, at, n)
        out[:, pl.ds(at, n)] = a.astype(BF)
        out[:, pl.ds(pl.multiple_of(feats + at, n), n)] = b.astype(BF)


def place(k, rows):
    y = lax.axis_index("block") // NC
    return pl.ds(pl.multiple_of(lax.rem(y + k + NY, NY) * rows, rows), rows)


def mine_kernel(hidden, grad, w1, w2, width, got, out):
    n, feats = 512, w1.shape[1]
    half = hidden.shape[0] // 2
    rows = half // 4

    @pl.loop(0, feats // n)
    def _(j):
        at = pl.multiple_of(j * n, n)
        pair = parts_of(pl.ds(0, half), hidden, grad, w1, w2, width, at, n)
        for k, part in enumerate(pair):
            to = pl.ds(pl.multiple_of(k * feats + at, n), n)
            part = (part + got[:, to].astype(F32)).astype(BF)
            for r, k in enumerate(ORDER):
                out[place(k, rows), to] = part[r * rows : (r + 1) * rows]


def terms_kernel(*refs):
    (mx, ox, mdy, ody, me, oe, width), refs = refs[:7], refs[7:]
    hs, gs, (far, up, down, rest), (left, right, acc) = refs[:4], refs[4:8], refs[8:12], refs[12:]
    dp = lax.axis_index("dp")
    x, z = dp // NZ, lax.rem(dp, NZ)
    rows = mx.shape[0]
    part = rows // NY
    quarter = mx.shape[1] // NX
    units = right.shape[1]
    own = pl.ds(pl.multiple_of(x * quarter, quarter), quarter)
    mask = live(width, x * quarter, quarter, BF)
    for which, (mine, other, hid) in enumerate(((mx, ox, gs), (mdy, ody, hs))):
        left[:rows, :] = mine[:, own] * mask
        left[rows : 2 * rows, :] = other[:, own] * mask
        for k in range(3):
            at = (2 * k + which) * quarter
            for half, got in enumerate((me, oe)):
                for r, step in enumerate(ORDER):
                    to = (2 * k + 2 + half) * rows + r * part
                    left[to : to + part, :] = got[place(step, part), at : at + quarter]
        for k in range(4):
            right[2 * k * rows : 2 * (k + 1) * rows, :] = hid[k][...]

        @pl.loop(0, quarter // 256)
        def _(j):
            term = dot(left[:, pl.ds(pl.multiple_of(j * 256, 256), 256)], right[...], 0, 0)
            acc[2 * j, :, which * units : (which + 1) * units] = term[:128]
            acc[2 * j + 1, :, which * units : (which + 1) * units] = term[128:]

    def pick(k):
        return acc[lax.rem(z + k + NZ, NZ)]

    n = acc.shape[1]
    far[...] = pick(4).astype(BF)
    up[:n, :] = pick(3).astype(BF)
    up[n:, :] = pick(1).astype(BF)
    down[:n, :] = pick(-3).astype(BF)
    down[n:, :] = pick(-1).astype(BF)
    for r, k in enumerate((2, -2, 0)):
        rest[r] = pick(k)


def middle_kernel(rest, up, down, low, high, up_far, down_far):
    half = low.shape[0]
    n = 2 * half
    up_far[:half, :] = (rest[0, :half] + up[:half, :].astype(F32) + low[...].astype(F32)).astype(BF)
    up_far[half:, :] = (rest[0, half:] + up[half:n, :].astype(F32)).astype(BF)
    down_far[:half, :] = (rest[1, :half] + down[:half, :].astype(F32)).astype(BF)
    down_far[half:, :] = (rest[1, half:] + down[half:n, :].astype(F32) + high[...].astype(F32)).astype(BF)


def last_kernel(rest, up, down, up_far, down_far, counts, up_grad, down_grad):
    n = rest.shape[1]
    units = up_grad.shape[2]
    scale = 1.0 / counts[lax.axis_index("block")].astype(F32)
    total = rest[2] + up[n:, :].astype(F32) + down[n:, :].astype(F32)
    total = (total + up_far[...].astype(F32) + down_far[...].astype(F32)) * scale
    up_grad[0] = total[:, :units]
    down_grad[0] = total[:, units:].T


def rows_kernel(x, dy, parts, mixed, input_grad):
    rows, feats = x.shape[1:]
    total = sum(parts[k * rows : (k + 1) * rows, :].astype(F32) for k in range(NY))
    mixed[0] = (x[0].astype(F32) + total[:, :feats]).astype(BF)
    input_grad[0] = (dy[0].astype(F32) + total[:, feats:]).astype(BF)


def local(tokens, cotangent, w_up, w_down, active, width, counts):
    rows, feats = tokens.shape[1:]
    units = w_up.shape[2]
    quarter = feats // NX
    v = lambda *arrays: [(array, VM) for array in arrays]
    s = lambda *arrays: [(array, SM) for array in arrays]
    mib = 2**20

    near_x = near(to_y, tokens[0])
    chunks = call(
        quarter_kernel, v(tokens, cotangent) + s(width), [((rows, 2 * quarter), BF)] * 3, 0, mib
    )
    near_dy = near(to_y, cotangent[0], near_x)
    extra = jnp.concatenate([to_x(c, k) for c, k in zip(chunks, (1, 2, -1))], axis=1)
    mine_x = jnp.concatenate([tokens[0]] + near_x, axis=0)
    other_x = to_core(then(mine_x, extra))
    mine_e = swap_y(jnp.concatenate([then(extra, near_dy[0])] * NY, axis=0))
    mine_dy = jnp.concatenate([cotangent[0]] + near_dy, axis=0)
    other_dy = to_core(mine_dy)

    big = 2 * 8 * rows * feats * units
    pair = [((8 * rows, units), BF), ((8 * rows, units), F32)]
    total = pltpu.VMEM((8 * rows, units), F32)
    hidden, slope = call(
        hidden_kernel, v(mine_x, other_x, w_up) + s(width, active), pair, big, 7 * mib, [total]
    )
    hidden_x = [hidden] + near(to_x, hidden)
    other_dy = then(other_dy, (hidden_x[1], hidden_x[3]))
    (grad,) = call(
        grad_kernel, v(mine_dy, other_dy, w_down) + s(width) + v(slope), pair[:1], big, 7 * mib, [total]
    )
    grad_x = [grad] + near(to_x, grad, hidden_x[1:])

    weights = v(hidden, grad, w_up, w_down) + s(width)
    (others,) = call(other_kernel, weights, [((4 * rows, 2 * feats), BF)], big, 10 * mib)
    got = then(to_core(others), hidden_x[2])
    (parts,) = call(mine_kernel, weights + v(got), [((4 * rows, 2 * feats), BF)], big, 12 * mib)
    mixed, input_grad = call(
        rows_kernel, v(tokens, cotangent, swap_y(parts)), [((1, rows, feats), BF)] * 2, 0, 3 * mib
    )
    other_e = to_core(then(mine_e, parts))

    n = quarter // NZ
    far, up, down, rest = call(
        terms_kernel,
        v(mine_x, other_x, mine_dy, other_dy, mine_e, other_e) + s(width) + v(*hidden_x, *grad_x),
        [((n, 2 * units), BF), ((2 * n, 2 * units), BF), ((2 * n, 2 * units), BF), ((3, n, 2 * units), F32)],
        2 * big,
        12 * mib,
        [
            pltpu.VMEM((NX * 8 * rows, quarter), BF),
            pltpu.VMEM((NX * 8 * rows, units), BF),
            pltpu.VMEM((NZ, n, 2 * units), F32),
        ],
    )
    low, high = to_z(far[: n // 2], 2), to_z(far[n // 2 :], -2)
    up, down = to_z(up, 1), to_z(down, -1)
    up_far, down_far = call(
        middle_kernel, v(rest, up, down, low, high), [((n, 2 * units), BF)] * 2, 0, 3 * mib
    )
    up_far, down_far = to_z(up_far, 2), to_z(down_far, -2)
    up_grad, down_grad = call(
        last_kernel,
        v(rest, up, down, up_far, down_far) + s(counts),
        [((1, n, units), F32), ((1, units, n), F32)],
        0,
        3 * mib,
    )
    return (mixed, input_grad, up_grad, down_grad)


def solution(mesh):
    in_specs = (
        P("dp", "block", None),
        P("dp", "block", None),
        P("block", None, None),
        P("block", None, None),
        P(),
        P(),
        P(),
    )
    out_specs = (
        P("dp", "block", None),
        P("dp", "block", None),
        P("block", "dp", None),
        P("block", None, "dp"),
    )
    return jax.shard_map(local, mesh=mesh, in_specs=in_specs, out_specs=out_specs, check_vma=False)
```

```python
import math

import jax
import jax.numpy as jnp
from jax import lax
from jax.experimental import pallas as pl
from jax.experimental.pallas import tpu as pltpu
from jax.sharding import PartitionSpec as P

GELU_C = math.sqrt(2.0 / math.pi)
NX, NZ, NY, NC = 4, 8, 4, 2
BF = jnp.bfloat16
F32 = jnp.float32


def gelu_parts(pre_vals):
    tanh_val = jnp.tanh(GELU_C * (pre_vals + 0.044715 * pre_vals * pre_vals * pre_vals))
    gelu_value = 0.5 * pre_vals * (1.0 + tanh_val)
    gelu_slope = 0.5 * (1.0 + tanh_val) + 0.5 * pre_vals * (1.0 - tanh_val * tanh_val) * GELU_C * (
        1.0 + 3.0 * 0.044715 * pre_vals * pre_vals
    )
    return (gelu_value, gelu_slope)


def to_y(v, k):
    return lax.ppermute(v, "block", [(i, (i + 2 * k) % 8) for i in range(8)])


def to_core(v):
    return lax.ppermute(v, "block", [(i, i ^ 1) for i in range(8)])


def to_x(v, k):
    return lax.ppermute(v, "dp", [(i, ((i // NZ + k) % NX) * NZ + i % NZ) for i in range(NX * NZ)])


def to_z(v, k):
    return lax.ppermute(v, "dp", [(i, (i // NZ) * NZ + (i % NZ + k) % NZ) for i in range(NX * NZ)])


VM = pl.BlockSpec(memory_space=pltpu.VMEM)
HB = pl.BlockSpec(memory_space=pl.ANY)
SM = pl.BlockSpec(memory_space=pltpu.SMEM)
WSTEP = 256


def call(kernel, ins, outs, scratch=(), mib=24):
    return pl.pallas_call(
        kernel,
        out_shape=[jax.ShapeDtypeStruct(shape, kind) for shape, kind in outs],
        in_specs=[spec for _, spec in ins],
        out_specs=[VM for _ in outs],
        scratch_shapes=list(scratch),
        compiler_params=pltpu.CompilerParams(vmem_limit_bytes=mib * 2**20),
        cost_estimate=pl.CostEstimate(flops=1, bytes_accessed=1, transcendentals=0),
    )(*[v for v, _ in ins])


def fetch(sources, sems):
    copies = [pltpu.make_async_copy(a, b, sems.at[k]) for k, (a, b) in enumerate(sources)]
    for copy in copies:
        copy.start()
    return copies


def near(send, v, after=(None, None, None)):
    return [send(then(v, a), k) for k, a in zip((1, 2, -1), after)]


def ring(send, v):
    half = v.shape[0] // 2
    before, after = send(v, 1), send(v, -1)
    return [before, send(before[:half], 1), send(after[half:], -1), after]


def then(v, after):
    return v if after is None else lax.optimization_barrier((v, after))[0]


def dot(a, b, ca, cb):
    return lax.dot_general(a, b, (((ca,), (cb,)), ((), ())), preferred_element_type=F32)


def live(width, at, n, kind):
    limit = WSTEP * width[lax.axis_index("dp")]
    return (at + lax.broadcasted_iota(jnp.int32, (1, n), 1) < limit).astype(F32).astype(kind)


def quarter_kernel(x_ref, dy_ref, width, a, b, c, x_own, dy_own, sems):
    for copy in fetch([(x_ref.at[0], x_own), (dy_ref.at[0], dy_own)], sems):
        copy.wait()
    quarter = x_own.shape[1] // NX
    x = lax.axis_index("dp") // NZ
    for out, k in zip((a, b, c), (1, 2, -1)):
        at = pl.multiple_of(lax.rem(x + k + NX, NX) * quarter, quarter)
        mask = live(width, at, quarter, BF)
        out[:, :quarter] = x_own[:, pl.ds(at, quarter)] * mask
        out[:, quarter:] = dy_own[:, pl.ds(at, quarter)] * mask


def masked_rows(mine, other, width, at, n):
    rows = jnp.concatenate([mine[:, at : at + n], other[:, at : at + n]], axis=0)
    return rows * live(width, at, n, BF)


CHUNKS = 4


def hidden_kernel(mine, other, w1, width, active, hidden, slope, held, sems):
    n = mine.shape[1] // CHUNKS
    cuts = [j * n for j in range(CHUNKS)]
    copies = fetch([(w1.at[0, pl.ds(at, n), :], held.at[pl.ds(at, n), :]) for at in cuts], sems)
    pre = 0.0
    for at, copy in zip(cuts, copies):
        copy.wait()
        pre += dot(masked_rows(mine, other, width, at, n), held[at : at + n, :], 1, 0)
    slope[...] = pre
    gate = active[lax.axis_index("block"), lax.axis_index("dp")].astype(F32)
    rows = 32

    @pl.loop(0, slope.shape[0] // rows)
    def _(j):
        at = pl.ds(pl.multiple_of(j * rows, rows), rows)
        value, grad = gelu_parts(slope[at, :])
        hidden[at, :] = (value * gate).astype(BF)
        slope[at, :] = grad * gate


def grad_kernel(mine, other, w2, width, hidden, slope, both, held, sems):
    n = mine.shape[1] // CHUNKS
    units = hidden.shape[1]
    cuts = [j * n for j in range(CHUNKS)]
    copies = fetch([(w2.at[0, :, pl.ds(at, n)], held.at[:, pl.ds(at, n)]) for at in cuts], sems)
    both[:, :units] = hidden[...]
    back = 0.0
    for at, copy in zip(cuts, copies):
        copy.wait()
        back += dot(masked_rows(mine, other, width, at, n), held[:, at : at + n], 1, 1)
    both[:, units:] = (back * slope[...]).astype(BF)


def out_kernel(hidden, w2, width, out, held, sems):
    n = out.shape[1] // CHUNKS
    cuts = [j * n for j in range(CHUNKS)]
    copies = fetch([(w2.at[0, :, pl.ds(at, n)], held.at[:, pl.ds(at, n)]) for at in cuts], sems)
    for at, copy in zip(cuts, copies):
        copy.wait()
        part = dot(hidden[...], held[:, at : at + n], 1, 0) * live(width, at, n, F32)
        out[:, at : at + n] = part.astype(BF)


def in_kernel(both, w1, out, width, mine, other, held, sems):
    feats, units = w1.shape[1:]
    n = feats // CHUNKS
    half = mine.shape[0]
    cuts = [j * n for j in range(CHUNKS)]
    copies = fetch([(w1.at[0, pl.ds(at, n), :], held.at[pl.ds(at, n), :]) for at in cuts], sems)
    mine[:, :feats] = out[:half, :]
    other[:, :feats] = out[half:, :]
    for at, copy in zip(cuts, copies):
        copy.wait()
        part = dot(both[:, units:], held[at : at + n, :], 1, 1) * live(width, at, n, F32)
        mine[:, feats + at : feats + at + n] = part[:half].astype(BF)
        other[:, feats + at : feats + at + n] = part[half:].astype(BF)


def pair_kernel(mine, got, *outs):
    rows = mine.shape[0] // NY
    for r, out in enumerate(outs):
        at = slice(r * rows, (r + 1) * rows)
        out[...] = (mine[at, :].astype(F32) + got[at, :].astype(F32)).astype(BF)


def pass_kernel(before, after, low, high, before_out, after_out):
    half = low.shape[0]
    after_out[:half, :] = (after[:half, :].astype(F32) + low[...].astype(F32)).astype(BF)
    after_out[half:, :] = after[half:, :]
    before_out[:half, :] = before[:half, :]
    before_out[half:, :] = (before[half:, :].astype(F32) + high[...].astype(F32)).astype(BF)


def terms_kernel(*refs):
    ins, width, hgs, refs = refs[:6], refs[6], refs[7:12], refs[12:]
    far, up, down, mid, own, left, right, acc, sems = refs
    dp = lax.axis_index("dp")
    x, z = dp // NZ, lax.rem(dp, NZ)
    rows = ins[0].shape[0]
    quarter = ins[0].shape[1] // NX
    units = right.shape[2]
    at = pl.ds(pl.multiple_of(x * quarter, quarter), quarter)
    jobs = []
    for which, (mine, other) in enumerate(((ins[2], ins[3]), (ins[0], ins[1]))):
        jobs += [
            (mine.at[:, at], left.at[which, pl.ds(0, rows), :]),
            (other.at[:, at], left.at[which, pl.ds(rows, rows), :]),
        ]
        for k in range(3):
            cut = pl.ds((2 * k + 1 - which) * quarter, quarter)
            for half in range(2):
                to = pl.ds((2 * k + 2 + half) * rows, rows)
                jobs.append((ins[4 + half].at[:, cut], left.at[which, to, :]))
        to = 0
        for piece in hgs:
            n = piece.shape[0]
            cols = pl.ds(which * units, units)
            jobs.append((piece.at[:, cols], right.at[which, pl.ds(to, n), :]))
            to += n
    copies = fetch(jobs, sems)
    mask = live(width, x * quarter, quarter, BF)
    count = len(copies) // 2
    for which in range(2):
        for copy in copies[which * count : (which + 1) * count]:
            copy.wait()
        left[which, : 2 * rows, :] = left[which, : 2 * rows, :] * mask
        col = (1 - which) * units
        for j in range(quarter // 512):
            term = dot(left[which, :, j * 512 : (j + 1) * 512], right[which], 0, 0)
            for k in range(4):
                acc[4 * j + k, :, col : col + units] = term[128 * k : 128 * (k + 1)]

    def pick(k):
        return acc[lax.rem(z + k + NZ, NZ)]

    n = acc.shape[1]
    far[...] = pick(4).astype(BF)
    up[:n, :] = pick(3).astype(BF)
    up[n:, :] = pick(1).astype(BF)
    down[:n, :] = pick(-3).astype(BF)
    down[n:, :] = pick(-1).astype(BF)
    mid[0] = pick(2)
    mid[1] = pick(-2)
    own[...] = pick(0)


def middle_kernel(mid, up, down, low, high, up_far, down_far):
    half = low.shape[0]
    n = 2 * half
    up_far[:half, :] = (mid[0, :half] + up[:half, :].astype(F32) + low[...].astype(F32)).astype(BF)
    up_far[half:, :] = (mid[0, half:] + up[half:n, :].astype(F32)).astype(BF)
    down_far[:half, :] = (mid[1, :half] + down[:half, :].astype(F32)).astype(BF)
    down_far[half:, :] = (mid[1, half:] + down[half:n, :].astype(F32) + high[...].astype(F32)).astype(BF)


def last_kernel(own, up, down, up_far, down_far, counts, up_grad, down_grad):
    n = own.shape[0]
    units = up_grad.shape[2]
    scale = 1.0 / counts[lax.axis_index("block")].astype(F32)
    total = own[...] + up[n:, :].astype(F32) + down[n:, :].astype(F32)
    total = (total + up_far[...].astype(F32) + down_far[...].astype(F32)) * scale
    up_grad[0] = total[:, :units]
    down_grad[0] = total[:, units:].T


def rows_kernel(x, dy, own, below, above, mixed, input_grad):
    feats = x.shape[2]
    total = own[...].astype(F32) + below[...].astype(F32) + above[...].astype(F32)
    mixed[0] = (x[0].astype(F32) + total[:, :feats]).astype(BF)
    input_grad[0] = (dy[0].astype(F32) + total[:, feats:]).astype(BF)


def local(tokens, cotangent, w_up, w_down, active, width, counts):
    rows, feats = tokens.shape[1:]
    units = w_up.shape[2]
    quarter = feats // NX
    n = quarter // NZ
    v = lambda *arrays: [(array, VM) for array in arrays]
    h = lambda *arrays: [(array, HB) for array in arrays]
    s = lambda *arrays: [(array, SM) for array in arrays]
    sems = lambda k: pltpu.SemaphoreType.DMA((k,))

    together = lambda *arrays: lax.optimization_barrier(arrays)

    pair = jnp.concatenate([tokens[0], cotangent[0]], axis=0)
    near_b = near(to_y, pair)
    chunks = call(
        quarter_kernel,
        h(tokens, cotangent) + s(width),
        [((rows, 2 * quarter), BF)] * 3,
        [pltpu.VMEM((rows, feats), BF)] * 2 + [sems(2)],
        56,
    )
    swapped = [to_x(c, k) for c, k in zip(chunks, (1, 2, -1))]
    pair, *got = together(pair, *swapped, *near_b)
    extra, near_b = jnp.concatenate(got[:3], axis=1), got[3:]

    mine_x = jnp.concatenate([b[:rows] for b in [pair] + near_b], axis=0)
    other_x = to_core(mine_x)
    mine_dy = jnp.concatenate([b[rows:] for b in [pair] + near_b], axis=0)
    other_dy = to_core(mine_dy)
    before, after = to_y(extra, 1), to_y(extra, -1)
    held_up = pltpu.VMEM((feats, units), BF)
    held_down = pltpu.VMEM((units, feats), BF)
    hidden, slope = call(
        hidden_kernel,
        v(mine_x, other_x) + h(w_up) + s(width, active.T),
        [((8 * rows, units), BF), ((8 * rows, units), F32)],
        [held_up, sems(CHUNKS)],
        50,
    )
    (out,) = call(
        out_kernel,
        v(hidden) + h(w_down) + s(width),
        [((8 * rows, feats), BF)],
        [held_down, sems(CHUNKS)],
        24,
    )
    hidden, slope, other_dy, before, after, out = together(
        hidden, slope, other_dy, before, after, out
    )

    (both,) = call(
        grad_kernel,
        v(mine_dy, other_dy) + h(w_down) + s(width) + v(hidden, slope),
        [((8 * rows, 2 * units), BF)],
        [held_down, sems(CHUNKS)],
        24,
    )
    left, right = to_x(both, 1), to_x(both, -1)
    half = rows // 2
    far = [to_y(before[:half], 1), to_y(after[half:], -1)]
    mine_e = jnp.concatenate([extra, before, *far, after], axis=0)
    mine, other = call(
        in_kernel,
        v(both) + h(w_up) + v(out) + s(width),
        [((4 * rows, 2 * feats), BF)] * 2,
        [held_up, sems(CHUNKS)],
        24,
    )
    both, left, right, mine_e, mine, other = together(both, left, right, mine_e, mine, other)

    both_x = [left, to_x(left[: 4 * rows], 1), to_x(right[4 * rows :], -1), right]
    other_e = to_core(mine_e)
    got = to_core(other)
    parts = call(pair_kernel, v(mine, got), [((rows, 2 * feats), BF)] * 4)
    both_x[1], both_x[2], other_e, *parts = together(both_x[1], both_x[2], other_e, *parts)
    sum_own, sum_before, sum_far, sum_after = parts
    sum_low, sum_high = to_y(sum_far[:half], 1), to_y(sum_far[half:], -1)

    far, up, down, mid, own = call(
        terms_kernel,
        h(mine_x, other_x, mine_dy, other_dy, mine_e, other_e) + s(width) + h(both, *both_x),
        [((n, 2 * units), BF), ((2 * n, 2 * units), BF), ((2 * n, 2 * units), BF)]
        + [((2, n, 2 * units), F32), ((n, 2 * units), F32)],
        [
            pltpu.VMEM((2, NX * 8 * rows, quarter), BF),
            pltpu.VMEM((2, NX * 8 * rows, units), BF),
            pltpu.VMEM((NZ, n, 2 * units), F32),
            sems(26),
        ],
    )
    far, sum_low, sum_high = together(far, sum_low, sum_high)
    low, high = to_z(far[: n // 2], 2), to_z(far[n // 2 :], -2)
    up, down = to_z(up, 1), to_z(down, -1)
    low, high, up, down = together(low, high, up, down)
    up_far, down_far = call(
        middle_kernel, v(mid, up, down, low, high), [((n, 2 * units), BF)] * 2
    )
    up_far, down_far = to_z(up_far, 2), to_z(down_far, -2)
    up_grad, down_grad = call(
        last_kernel,
        v(own, up, down, up_far, down_far) + s(counts),
        [((1, n, units), F32), ((1, units, n), F32)],
    )
    sum_before, sum_after = call(
        pass_kernel, v(sum_before, sum_after, sum_low, sum_high), [((rows, 2 * feats), BF)] * 2
    )
    mixed, input_grad = call(
        rows_kernel, v(tokens, cotangent, sum_own, to_y(sum_after, 1), to_y(sum_before, -1)), [((1, rows, feats), BF)] * 2
    )
    return (mixed, input_grad, up_grad, down_grad)


def solution(mesh):
    in_specs = (
        P("dp", "block", None),
        P("dp", "block", None),
        P("block", None, None),
        P("block", None, None),
        P(),
        P(),
        P(),
    )
    out_specs = (
        P("dp", "block", None),
        P("dp", "block", None),
        P("block", "dp", None),
        P("block", None, "dp"),
    )
    return jax.shard_map(local, mesh=mesh, in_specs=in_specs, out_specs=out_specs, check_vma=False)
```

```python
import math

import jax
import jax.numpy as jnp
from jax import lax
from jax.experimental import pallas as pl
from jax.experimental.pallas import tpu as pltpu
from jax.sharding import PartitionSpec as P

GELU_C = math.sqrt(2.0 / math.pi)
NX, NZ, NY, NC = 4, 8, 4, 2
BF = jnp.bfloat16
F32 = jnp.float32


def gelu_parts(pre_vals):
    tanh_val = jnp.tanh(GELU_C * (pre_vals + 0.044715 * pre_vals * pre_vals * pre_vals))
    gelu_value = 0.5 * pre_vals * (1.0 + tanh_val)
    gelu_slope = 0.5 * (1.0 + tanh_val) + 0.5 * pre_vals * (1.0 - tanh_val * tanh_val) * GELU_C * (
        1.0 + 3.0 * 0.044715 * pre_vals * pre_vals
    )
    return (gelu_value, gelu_slope)


def to_y(v, k):
    return lax.ppermute(v, "block", [(i, (i + 2 * k) % 8) for i in range(8)])


def to_core(v):
    return lax.ppermute(v, "block", [(i, i ^ 1) for i in range(8)])


def to_x(v, k):
    return lax.ppermute(v, "dp", [(i, ((i // NZ + k) % NX) * NZ + i % NZ) for i in range(NX * NZ)])


def to_z(v, k):
    return lax.ppermute(v, "dp", [(i, (i // NZ) * NZ + (i % NZ + k) % NZ) for i in range(NX * NZ)])


VM = pl.BlockSpec(memory_space=pltpu.VMEM)
HB = pl.BlockSpec(memory_space=pl.ANY)
SM = pl.BlockSpec(memory_space=pltpu.SMEM)
WSTEP = 256


def call(kernel, ins, outs, scratch=(), mib=24):
    return pl.pallas_call(
        kernel,
        out_shape=[jax.ShapeDtypeStruct(shape, kind) for shape, kind in outs],
        in_specs=[spec for _, spec in ins],
        out_specs=[VM for _ in outs],
        scratch_shapes=list(scratch),
        compiler_params=pltpu.CompilerParams(vmem_limit_bytes=mib * 2**20),
        cost_estimate=pl.CostEstimate(flops=1, bytes_accessed=1, transcendentals=0),
    )(*[v for v, _ in ins])


def fetch(sources, sems):
    copies = [pltpu.make_async_copy(a, b, sems.at[k]) for k, (a, b) in enumerate(sources)]
    for copy in copies:
        copy.start()
    return copies


def near(send, v, after=(None, None, None)):
    return [send(then(v, a), k) for k, a in zip((1, 2, -1), after)]


def ring(send, v):
    half = v.shape[0] // 2
    before, after = send(v, 1), send(v, -1)
    return [before, send(before[:half], 1), send(after[half:], -1), after]


def then(v, after):
    return v if after is None else lax.optimization_barrier((v, after))[0]


def dot(a, b, ca, cb):
    return lax.dot_general(a, b, (((ca,), (cb,)), ((), ())), preferred_element_type=F32)


def live(width, at, n, kind):
    limit = WSTEP * width[lax.axis_index("dp")]
    return (at + lax.broadcasted_iota(jnp.int32, (1, n), 1) < limit).astype(F32).astype(kind)


def quarter_kernel(x_ref, dy_ref, width, a, b, c, x_own, dy_own, sems):
    for copy in fetch([(x_ref.at[0], x_own), (dy_ref.at[0], dy_own)], sems):
        copy.wait()
    quarter = x_own.shape[1] // NX
    x = lax.axis_index("dp") // NZ
    for out, k in zip((a, b, c), (1, 2, -1)):
        at = pl.multiple_of(lax.rem(x + k + NX, NX) * quarter, quarter)
        mask = live(width, at, quarter, BF)
        out[:, :quarter] = x_own[:, pl.ds(at, quarter)] * mask
        out[:, quarter:] = dy_own[:, pl.ds(at, quarter)] * mask


def masked_rows(mine, other, width, at, n):
    rows = jnp.concatenate([mine[:, at : at + n], other[:, at : at + n]], axis=0)
    return rows * live(width, at, n, BF)


CHUNKS = 4


def hidden_kernel(mine, other, w1, width, active, hidden, slope, held, sems):
    n = mine.shape[1] // CHUNKS
    cuts = [j * n for j in range(CHUNKS)]
    copies = fetch([(w1.at[0, pl.ds(at, n), :], held.at[pl.ds(at, n), :]) for at in cuts], sems)
    pre = 0.0
    for at, copy in zip(cuts, copies):
        copy.wait()
        pre += dot(masked_rows(mine, other, width, at, n), held[at : at + n, :], 1, 0)
    slope[...] = pre
    gate = active[lax.axis_index("block"), lax.axis_index("dp")].astype(F32)
    rows = 32

    @pl.loop(0, slope.shape[0] // rows)
    def _(j):
        at = pl.ds(pl.multiple_of(j * rows, rows), rows)
        value, grad = gelu_parts(slope[at, :])
        hidden[at, :] = (value * gate).astype(BF)
        slope[at, :] = grad * gate


def grad_kernel(mine, other, w2, width, hidden, slope, both, held, sems):
    n = mine.shape[1] // CHUNKS
    units = hidden.shape[1]
    cuts = [j * n for j in range(CHUNKS)]
    copies = fetch([(w2.at[0, :, pl.ds(at, n)], held.at[:, pl.ds(at, n)]) for at in cuts], sems)
    both[:, :units] = hidden[...]
    back = 0.0
    for at, copy in zip(cuts, copies):
        copy.wait()
        back += dot(masked_rows(mine, other, width, at, n), held[:, at : at + n], 1, 1)
    both[:, units:] = (back * slope[...]).astype(BF)


def out_kernel(hidden, w2, width, out, held, sems):
    n = out.shape[1] // CHUNKS
    cuts = [j * n for j in range(CHUNKS)]
    copies = fetch([(w2.at[0, :, pl.ds(at, n)], held.at[:, pl.ds(at, n)]) for at in cuts], sems)
    for at, copy in zip(cuts, copies):
        copy.wait()
        part = dot(hidden[...], held[:, at : at + n], 1, 0) * live(width, at, n, F32)
        out[:, at : at + n] = part.astype(BF)


def in_kernel(both, w1, out, width, mine, other, held, sems):
    feats, units = w1.shape[1:]
    n = feats // CHUNKS
    half = mine.shape[0]
    cuts = [j * n for j in range(CHUNKS)]
    copies = fetch([(w1.at[0, pl.ds(at, n), :], held.at[pl.ds(at, n), :]) for at in cuts], sems)
    mine[:, :feats] = out[:half, :]
    other[:, :feats] = out[half:, :]
    for at, copy in zip(cuts, copies):
        copy.wait()
        part = dot(both[:, units:], held[at : at + n, :], 1, 1) * live(width, at, n, F32)
        mine[:, feats + at : feats + at + n] = part[:half].astype(BF)
        other[:, feats + at : feats + at + n] = part[half:].astype(BF)


def pair_kernel(mine, got, *outs):
    rows = mine.shape[0] // NY
    for r, out in enumerate(outs):
        at = slice(r * rows, (r + 1) * rows)
        out[...] = (mine[at, :].astype(F32) + got[at, :].astype(F32)).astype(BF)


def pass_kernel(before, after, low, high, before_out, after_out):
    half = low.shape[0]
    after_out[:half, :] = (after[:half, :].astype(F32) + low[...].astype(F32)).astype(BF)
    after_out[half:, :] = after[half:, :]
    before_out[:half, :] = before[:half, :]
    before_out[half:, :] = (before[half:, :].astype(F32) + high[...].astype(F32)).astype(BF)


def terms_kernel(*refs):
    ins, width, hgs, refs = refs[:6], refs[6], refs[7:12], refs[12:]
    far, up, down, mid, own, left, right, acc, sems = refs
    dp = lax.axis_index("dp")
    x, z = dp // NZ, lax.rem(dp, NZ)
    rows = ins[0].shape[0]
    quarter = ins[0].shape[1] // NX
    units = right.shape[2]
    at = pl.ds(pl.multiple_of(x * quarter, quarter), quarter)
    jobs = []
    for which, (mine, other) in enumerate(((ins[2], ins[3]), (ins[0], ins[1]))):
        jobs += [
            (mine.at[:, at], left.at[which, pl.ds(0, rows), :]),
            (other.at[:, at], left.at[which, pl.ds(rows, rows), :]),
        ]
        for k in range(3):
            cut = pl.ds((2 * k + 1 - which) * quarter, quarter)
            for half in range(2):
                to = pl.ds((2 * k + 2 + half) * rows, rows)
                jobs.append((ins[4 + half].at[:, cut], left.at[which, to, :]))
        to = 0
        for piece in hgs:
            n = piece.shape[0]
            cols = pl.ds(which * units, units)
            jobs.append((piece.at[:, cols], right.at[which, pl.ds(to, n), :]))
            to += n
    copies = fetch(jobs, sems)
    mask = live(width, x * quarter, quarter, BF)
    count = len(copies) // 2
    for which in range(2):
        for copy in copies[which * count : (which + 1) * count]:
            copy.wait()
        left[which, : 2 * rows, :] = left[which, : 2 * rows, :] * mask
        col = (1 - which) * units
        for j in range(quarter // 512):
            term = dot(left[which, :, j * 512 : (j + 1) * 512], right[which], 0, 0)
            for k in range(4):
                acc[4 * j + k, :, col : col + units] = term[128 * k : 128 * (k + 1)]

    def pick(k):
        return acc[lax.rem(z + k + NZ, NZ)]

    n = acc.shape[1]
    far[...] = pick(4).astype(BF)
    up[:n, :] = pick(3).astype(BF)
    up[n:, :] = pick(1).astype(BF)
    down[:n, :] = pick(-3).astype(BF)
    down[n:, :] = pick(-1).astype(BF)
    mid[0] = pick(2)
    mid[1] = pick(-2)
    own[...] = pick(0)


def middle_kernel(mid, up, down, low, high, up_far, down_far):
    half = low.shape[0]
    n = 2 * half
    up_far[:half, :] = (mid[0, :half] + up[:half, :].astype(F32) + low[...].astype(F32)).astype(BF)
    up_far[half:, :] = (mid[0, half:] + up[half:n, :].astype(F32)).astype(BF)
    down_far[:half, :] = (mid[1, :half] + down[:half, :].astype(F32)).astype(BF)
    down_far[half:, :] = (mid[1, half:] + down[half:n, :].astype(F32) + high[...].astype(F32)).astype(BF)


def last_kernel(own, up, down, up_far, down_far, counts, up_grad, down_grad):
    n = own.shape[0]
    units = up_grad.shape[2]
    scale = 1.0 / counts[lax.axis_index("block")].astype(F32)
    total = own[...] + up[n:, :].astype(F32) + down[n:, :].astype(F32)
    total = (total + up_far[...].astype(F32) + down_far[...].astype(F32)) * scale
    up_grad[0] = total[:, :units]
    down_grad[0] = total[:, units:].T


def rows_kernel(x, dy, own, below, above, mixed, input_grad):
    feats = x.shape[2]
    total = own[...].astype(F32) + below[...].astype(F32) + above[...].astype(F32)
    mixed[0] = (x[0].astype(F32) + total[:, :feats]).astype(BF)
    input_grad[0] = (dy[0].astype(F32) + total[:, feats:]).astype(BF)


def local(tokens, cotangent, w_up, w_down, active, width, counts):
    rows, feats = tokens.shape[1:]
    units = w_up.shape[2]
    quarter = feats // NX
    n = quarter // NZ
    v = lambda *arrays: [(array, VM) for array in arrays]
    h = lambda *arrays: [(array, HB) for array in arrays]
    s = lambda *arrays: [(array, SM) for array in arrays]
    sems = lambda k: pltpu.SemaphoreType.DMA((k,))

    together = lambda *arrays: lax.optimization_barrier(arrays)

    pair = jnp.concatenate([tokens[0], cotangent[0]], axis=0)
    near_b = near(to_y, pair)
    chunks = call(
        quarter_kernel,
        h(tokens, cotangent) + s(width),
        [((rows, 2 * quarter), BF)] * 3,
        [pltpu.VMEM((rows, feats), BF)] * 2 + [sems(2)],
        56,
    )
    swapped = [to_x(c, k) for c, k in zip(chunks, (1, 2, -1))]
    pair, *got = together(pair, *swapped, *near_b)
    extra, near_b = jnp.concatenate(got[:3], axis=1), got[3:]

    mine_x = jnp.concatenate([b[:rows] for b in [pair] + near_b], axis=0)
    other_x = to_core(mine_x)
    mine_dy = jnp.concatenate([b[rows:] for b in [pair] + near_b], axis=0)
    other_dy = to_core(mine_dy)
    before, after = to_y(extra, 1), to_y(extra, -1)
    held_up = pltpu.VMEM((feats, units), BF)
    held_down = pltpu.VMEM((units, feats), BF)
    hidden, slope = call(
        hidden_kernel,
        v(mine_x, other_x) + h(w_up) + s(width, active.T),
        [((8 * rows, units), BF), ((8 * rows, units), F32)],
        [held_up, sems(CHUNKS)],
        50,
    )
    (out,) = call(
        out_kernel,
        v(hidden) + h(w_down) + s(width),
        [((8 * rows, feats), BF)],
        [held_down, sems(CHUNKS)],
        24,
    )
    hidden, slope, other_dy, before, after, out = together(
        hidden, slope, other_dy, before, after, out
    )

    (both,) = call(
        grad_kernel,
        v(mine_dy, other_dy) + h(w_down) + s(width) + v(hidden, slope),
        [((8 * rows, 2 * units), BF)],
        [held_down, sems(CHUNKS)],
        24,
    )
    left, right = to_x(both, 1), to_x(both, -1)
    half = rows // 2
    far = [to_y(before[:half], 1), to_y(after[half:], -1)]
    mine_e = jnp.concatenate([extra, before, *far, after], axis=0)
    mine, other = call(
        in_kernel,
        v(both) + h(w_up) + v(out) + s(width),
        [((4 * rows, 2 * feats), BF)] * 2,
        [held_up, sems(CHUNKS)],
        24,
    )
    both, left, right, mine_e, mine, other = together(both, left, right, mine_e, mine, other)

    both_x = [left, to_x(left[: 4 * rows], 1), to_x(right[4 * rows :], -1), right]
    other_e = to_core(mine_e)
    got = to_core(other)
    parts = call(pair_kernel, v(mine, got), [((rows, 2 * feats), BF)] * 4)
    both_x[1], both_x[2], other_e, *parts = together(both_x[1], both_x[2], other_e, *parts)
    sum_own, sum_before, sum_far, sum_after = parts
    sum_low, sum_high = to_y(sum_far[:half], 1), to_y(sum_far[half:], -1)

    far, up, down, mid, own = call(
        terms_kernel,
        h(mine_x, other_x, mine_dy, other_dy, mine_e, other_e) + s(width) + h(both, *both_x),
        [((n, 2 * units), BF), ((2 * n, 2 * units), BF), ((2 * n, 2 * units), BF)]
        + [((2, n, 2 * units), F32), ((n, 2 * units), F32)],
        [
            pltpu.VMEM((2, NX * 8 * rows, quarter), BF),
            pltpu.VMEM((2, NX * 8 * rows, units), BF),
            pltpu.VMEM((NZ, n, 2 * units), F32),
            sems(26),
        ],
    )
    far, sum_low, sum_high = together(far, sum_low, sum_high)
    low, high = to_z(far[: n // 2], 2), to_z(far[n // 2 :], -2)
    up, down = to_z(up, 1), to_z(down, -1)
    low, high, up, down = together(low, high, up, down)
    up_far, down_far = call(
        middle_kernel, v(mid, up, down, low, high), [((n, 2 * units), BF)] * 2
    )
    up_far, down_far = to_z(up_far, 2), to_z(down_far, -2)
    up_grad, down_grad = call(
        last_kernel,
        v(own, up, down, up_far, down_far) + s(counts),
        [((1, n, units), F32), ((1, units, n), F32)],
    )
    sum_before, sum_after = call(
        pass_kernel, v(sum_before, sum_after, sum_low, sum_high), [((rows, 2 * feats), BF)] * 2
    )
    mixed, input_grad = call(
        rows_kernel, v(tokens, cotangent, sum_own, to_y(sum_after, 1), to_y(then(sum_before, (low, high)), -1)), [((1, rows, feats), BF)] * 2
    )
    return (mixed, input_grad, up_grad, down_grad)


def solution(mesh):
    in_specs = (
        P("dp", "block", None),
        P("dp", "block", None),
        P("block", None, None),
        P("block", None, None),
        P(),
        P(),
        P(),
    )
    out_specs = (
        P("dp", "block", None),
        P("dp", "block", None),
        P("block", "dp", None),
        P("block", None, "dp"),
    )
    return jax.shard_map(local, mesh=mesh, in_specs=in_specs, out_specs=out_specs, check_vma=False)
```

```python
import math

import jax
import jax.numpy as jnp
from jax import lax
from jax.experimental import pallas as pl
from jax.experimental.pallas import tpu as pltpu
from jax.sharding import PartitionSpec as P

GELU_C = math.sqrt(2.0 / math.pi)
NX, NZ, NY, NC = 4, 8, 4, 2
BF = jnp.bfloat16
F32 = jnp.float32


def gelu_parts(pre_vals):
    tanh_val = jnp.tanh(GELU_C * (pre_vals + 0.044715 * pre_vals * pre_vals * pre_vals))
    gelu_value = 0.5 * pre_vals * (1.0 + tanh_val)
    gelu_slope = 0.5 * (1.0 + tanh_val) + 0.5 * pre_vals * (1.0 - tanh_val * tanh_val) * GELU_C * (
        1.0 + 3.0 * 0.044715 * pre_vals * pre_vals
    )
    return (gelu_value, gelu_slope)


def to_y(v, k):
    return lax.ppermute(v, "block", [(i, (i + 2 * k) % 8) for i in range(8)])


def to_core(v):
    return lax.ppermute(v, "block", [(i, i ^ 1) for i in range(8)])


def to_x(v, k):
    return lax.ppermute(v, "dp", [(i, ((i // NZ + k) % NX) * NZ + i % NZ) for i in range(NX * NZ)])


def to_z(v, k):
    return lax.ppermute(v, "dp", [(i, (i // NZ) * NZ + (i % NZ + k) % NZ) for i in range(NX * NZ)])


VM = pl.BlockSpec(memory_space=pltpu.VMEM)
HB = pl.BlockSpec(memory_space=pl.ANY)
SM = pl.BlockSpec(memory_space=pltpu.SMEM)
WSTEP = 256


def call(kernel, ins, outs, scratch=(), mib=24):
    return pl.pallas_call(
        kernel,
        out_shape=[jax.ShapeDtypeStruct(shape, kind) for shape, kind in outs],
        in_specs=[spec for _, spec in ins],
        out_specs=[VM for _ in outs],
        scratch_shapes=list(scratch),
        compiler_params=pltpu.CompilerParams(vmem_limit_bytes=mib * 2**20),
        cost_estimate=pl.CostEstimate(flops=1, bytes_accessed=1, transcendentals=0),
    )(*[v for v, _ in ins])


def fetch(sources, sems):
    copies = [pltpu.make_async_copy(a, b, sems.at[k]) for k, (a, b) in enumerate(sources)]
    for copy in copies:
        copy.start()
    return copies


def near(send, v, after=(None, None, None)):
    return [send(then(v, a), k) for k, a in zip((1, 2, -1), after)]


def ring(send, v):
    half = v.shape[0] // 2
    before, after = send(v, 1), send(v, -1)
    return [before, send(before[:half], 1), send(after[half:], -1), after]


def then(v, after):
    return v if after is None else lax.optimization_barrier((v, after))[0]


def dot(a, b, ca, cb):
    return lax.dot_general(a, b, (((ca,), (cb,)), ((), ())), preferred_element_type=F32)


def live(width, at, n, kind):
    limit = WSTEP * width[lax.axis_index("dp")]
    return (at + lax.broadcasted_iota(jnp.int32, (1, n), 1) < limit).astype(F32).astype(kind)


def quarter_kernel(x_ref, dy_ref, width, a, b, c, x_own, dy_own, sems):
    for copy in fetch([(x_ref.at[0], x_own), (dy_ref.at[0], dy_own)], sems):
        copy.wait()
    quarter = x_own.shape[1] // NX
    x = lax.axis_index("dp") // NZ
    for out, k in zip((a, b, c), (1, 2, -1)):
        at = pl.multiple_of(lax.rem(x + k + NX, NX) * quarter, quarter)
        mask = live(width, at, quarter, BF)
        out[:, :quarter] = x_own[:, pl.ds(at, quarter)] * mask
        out[:, quarter:] = dy_own[:, pl.ds(at, quarter)] * mask


def masked_rows(mine, other, width, at, n):
    rows = jnp.concatenate([mine[:, at : at + n], other[:, at : at + n]], axis=0)
    return rows * live(width, at, n, BF)


CHUNKS = 4


def hidden_kernel(mine, other, w1, width, active, hidden, slope, held, sems):
    n = mine.shape[1] // CHUNKS
    cuts = [j * n for j in range(CHUNKS)]
    copies = fetch([(w1.at[0, pl.ds(at, n), :], held.at[pl.ds(at, n), :]) for at in cuts], sems)
    pre = 0.0
    for at, copy in zip(cuts, copies):
        copy.wait()
        pre += dot(masked_rows(mine, other, width, at, n), held[at : at + n, :], 1, 0)
    slope[...] = pre
    gate = active[lax.axis_index("block"), lax.axis_index("dp")].astype(F32)
    rows = 32

    @pl.loop(0, slope.shape[0] // rows)
    def _(j):
        at = pl.ds(pl.multiple_of(j * rows, rows), rows)
        value, grad = gelu_parts(slope[at, :])
        hidden[at, :] = (value * gate).astype(BF)
        slope[at, :] = grad * gate


def grad_kernel(mine, other, w2, width, hidden, slope, both, held, sems):
    n = mine.shape[1] // CHUNKS
    units = hidden.shape[1]
    cuts = [j * n for j in range(CHUNKS)]
    copies = fetch([(w2.at[0, :, pl.ds(at, n)], held.at[:, pl.ds(at, n)]) for at in cuts], sems)
    both[:, :units] = hidden[...]
    back = 0.0
    for at, copy in zip(cuts, copies):
        copy.wait()
        back += dot(masked_rows(mine, other, width, at, n), held[:, at : at + n], 1, 1)
    both[:, units:] = (back * slope[...]).astype(BF)


def out_kernel(hidden, w2, width, out, held, sems):
    n = out.shape[1] // CHUNKS
    cuts = [j * n for j in range(CHUNKS)]
    copies = fetch([(w2.at[0, :, pl.ds(at, n)], held.at[:, pl.ds(at, n)]) for at in cuts], sems)
    for at, copy in zip(cuts, copies):
        copy.wait()
        part = dot(hidden[...], held[:, at : at + n], 1, 0) * live(width, at, n, F32)
        out[:, at : at + n] = part.astype(BF)


def in_kernel(both, w1, out, width, mine, other, held, sems):
    feats, units = w1.shape[1:]
    n = feats // CHUNKS
    half = mine.shape[0]
    cuts = [j * n for j in range(CHUNKS)]
    copies = fetch([(w1.at[0, pl.ds(at, n), :], held.at[pl.ds(at, n), :]) for at in cuts], sems)
    mine[:, :feats] = out[:half, :]
    other[:, :feats] = out[half:, :]
    for at, copy in zip(cuts, copies):
        copy.wait()
        part = dot(both[:, units:], held[at : at + n, :], 1, 1) * live(width, at, n, F32)
        mine[:, feats + at : feats + at + n] = part[:half].astype(BF)
        other[:, feats + at : feats + at + n] = part[half:].astype(BF)


def pair_kernel(mine, got, *outs):
    rows = mine.shape[0] // NY
    for r, out in enumerate(outs):
        at = slice(r * rows, (r + 1) * rows)
        out[...] = (mine[at, :].astype(F32) + got[at, :].astype(F32)).astype(BF)


def pass_kernel(before, after, low, high, before_out, after_out):
    half = low.shape[0]
    after_out[:half, :] = (after[:half, :].astype(F32) + low[...].astype(F32)).astype(BF)
    after_out[half:, :] = after[half:, :]
    before_out[:half, :] = before[:half, :]
    before_out[half:, :] = (before[half:, :].astype(F32) + high[...].astype(F32)).astype(BF)


def terms_kernel(*refs):
    ins, width, hgs, refs = refs[:6], refs[6], refs[7:12], refs[12:]
    far, up, down, mid, own, left, right, acc, sems = refs
    dp = lax.axis_index("dp")
    x, z = dp // NZ, lax.rem(dp, NZ)
    rows = ins[0].shape[0]
    quarter = ins[0].shape[1] // NX
    units = right.shape[2]
    at = pl.ds(pl.multiple_of(x * quarter, quarter), quarter)
    jobs = []
    for which, (mine, other) in enumerate(((ins[2], ins[3]), (ins[0], ins[1]))):
        jobs += [
            (mine.at[:, at], left.at[which, pl.ds(0, rows), :]),
            (other.at[:, at], left.at[which, pl.ds(rows, rows), :]),
        ]
        for k in range(3):
            cut = pl.ds((2 * k + 1 - which) * quarter, quarter)
            for half in range(2):
                to = pl.ds((2 * k + 2 + half) * rows, rows)
                jobs.append((ins[4 + half].at[:, cut], left.at[which, to, :]))
        to = 0
        for piece in hgs:
            n = piece.shape[0]
            cols = pl.ds(which * units, units)
            jobs.append((piece.at[:, cols], right.at[which, pl.ds(to, n), :]))
            to += n
    copies = fetch(jobs, sems)
    mask = live(width, x * quarter, quarter, BF)
    count = len(copies) // 2
    for which in range(2):
        for copy in copies[which * count : (which + 1) * count]:
            copy.wait()
        left[which, : 2 * rows, :] = left[which, : 2 * rows, :] * mask
        col = (1 - which) * units
        for j in range(quarter // 512):
            term = dot(left[which, :, j * 512 : (j + 1) * 512], right[which], 0, 0)
            for k in range(4):
                acc[4 * j + k, :, col : col + units] = term[128 * k : 128 * (k + 1)]

    def pick(k):
        return acc[lax.rem(z + k + NZ, NZ)]

    n = acc.shape[1]
    far[...] = pick(4).astype(BF)
    up[:n, :] = pick(3).astype(BF)
    up[n:, :] = pick(1).astype(BF)
    down[:n, :] = pick(-3).astype(BF)
    down[n:, :] = pick(-1).astype(BF)
    mid[0] = pick(2)
    mid[1] = pick(-2)
    own[...] = pick(0)


def middle_kernel(mid, up, down, low, high, up_far, down_far):
    half = low.shape[0]
    n = 2 * half
    up_far[:half, :] = (mid[0, :half] + up[:half, :].astype(F32) + low[...].astype(F32)).astype(BF)
    up_far[half:, :] = (mid[0, half:] + up[half:n, :].astype(F32)).astype(BF)
    down_far[:half, :] = (mid[1, :half] + down[:half, :].astype(F32)).astype(BF)
    down_far[half:, :] = (mid[1, half:] + down[half:n, :].astype(F32) + high[...].astype(F32)).astype(BF)


def last_kernel(own, up, down, up_far, down_far, counts, up_grad, down_grad):
    n = own.shape[0]
    units = up_grad.shape[2]
    scale = 1.0 / counts[lax.axis_index("block")].astype(F32)
    total = own[...] + up[n:, :].astype(F32) + down[n:, :].astype(F32)
    total = (total + up_far[...].astype(F32) + down_far[...].astype(F32)) * scale
    up_grad[0] = total[:, :units]
    down_grad[0] = total[:, units:].T


def rows_kernel(x, dy, own, below, above, mixed, input_grad):
    feats = x.shape[2]
    total = own[...].astype(F32) + below[...].astype(F32) + above[...].astype(F32)
    mixed[0] = (x[0].astype(F32) + total[:, :feats]).astype(BF)
    input_grad[0] = (dy[0].astype(F32) + total[:, feats:]).astype(BF)


def local(tokens, cotangent, w_up, w_down, active, width, counts):
    rows, feats = tokens.shape[1:]
    units = w_up.shape[2]
    quarter = feats // NX
    n = quarter // NZ
    v = lambda *arrays: [(array, VM) for array in arrays]
    h = lambda *arrays: [(array, HB) for array in arrays]
    s = lambda *arrays: [(array, SM) for array in arrays]
    sems = lambda k: pltpu.SemaphoreType.DMA((k,))

    together = lambda *arrays: lax.optimization_barrier(arrays)

    pair = jnp.concatenate([tokens[0], cotangent[0]], axis=0)
    near_b = near(to_y, pair)
    chunks = call(
        quarter_kernel,
        h(tokens, cotangent) + s(width),
        [((rows, 2 * quarter), BF)] * 3,
        [pltpu.VMEM((rows, feats), BF)] * 2 + [sems(2)],
        56,
    )
    swapped = [to_x(c, k) for c, k in zip(chunks, (1, 2, -1))]
    pair, *got = together(pair, *swapped, *near_b)
    extra, near_b = jnp.concatenate(got[:3], axis=1), got[3:]

    mine_x = jnp.concatenate([b[:rows] for b in [pair] + near_b], axis=0)
    other_x = to_core(mine_x)
    mine_dy = jnp.concatenate([b[rows:] for b in [pair] + near_b], axis=0)
    other_dy = to_core(mine_dy)
    before, after = to_y(extra, 1), to_y(extra, -1)
    held_up = pltpu.VMEM((feats, units), BF)
    held_down = pltpu.VMEM((units, feats), BF)
    hidden, slope = call(
        hidden_kernel,
        v(mine_x, other_x) + h(w_up) + s(width, active.T),
        [((8 * rows, units), BF), ((8 * rows, units), F32)],
        [held_up, sems(CHUNKS)],
        50,
    )
    (out,) = call(
        out_kernel,
        v(hidden) + h(w_down) + s(width),
        [((8 * rows, feats), BF)],
        [held_down, sems(CHUNKS)],
        24,
    )

    (both,) = call(
        grad_kernel,
        v(mine_dy, other_dy) + h(w_down) + s(width) + v(hidden, slope),
        [((8 * rows, 2 * units), BF)],
        [held_down, sems(CHUNKS)],
        24,
    )
    both, before, after, out = together(both, before, after, out)

    left, right = to_x(both, 1), to_x(both, -1)
    half = rows // 2
    far = [to_y(before[:half], 1), to_y(after[half:], -1)]
    mine_e = jnp.concatenate([extra, before, *far, after], axis=0)
    mine, other = call(
        in_kernel,
        v(both) + h(w_up) + v(out) + s(width),
        [((4 * rows, 2 * feats), BF)] * 2,
        [held_up, sems(CHUNKS)],
        24,
    )
    both, left, right, mine_e, mine, other = together(both, left, right, mine_e, mine, other)

    both_x = [left, to_x(left[: 4 * rows], 1), to_x(right[4 * rows :], -1), right]
    other_e = to_core(mine_e)
    got = to_core(other)
    parts = call(pair_kernel, v(mine, got), [((rows, 2 * feats), BF)] * 4)
    both_x[1], both_x[2], other_e, *parts = together(both_x[1], both_x[2], other_e, *parts)
    sum_own, sum_before, sum_far, sum_after = parts
    sum_low, sum_high = to_y(sum_far[:half], 1), to_y(sum_far[half:], -1)

    far, up, down, mid, own = call(
        terms_kernel,
        h(mine_x, other_x, mine_dy, other_dy, mine_e, other_e) + s(width) + h(both, *both_x),
        [((n, 2 * units), BF), ((2 * n, 2 * units), BF), ((2 * n, 2 * units), BF)]
        + [((2, n, 2 * units), F32), ((n, 2 * units), F32)],
        [
            pltpu.VMEM((2, NX * 8 * rows, quarter), BF),
            pltpu.VMEM((2, NX * 8 * rows, units), BF),
            pltpu.VMEM((NZ, n, 2 * units), F32),
            sems(26),
        ],
    )
    far, sum_low, sum_high = together(far, sum_low, sum_high)
    low, high = to_z(far[: n // 2], 2), to_z(far[n // 2 :], -2)
    up, down = to_z(up, 1), to_z(down, -1)
    low, high, up, down = together(low, high, up, down)
    up_far, down_far = call(
        middle_kernel, v(mid, up, down, low, high), [((n, 2 * units), BF)] * 2
    )
    up_far, down_far = to_z(up_far, 2), to_z(down_far, -2)
    up_grad, down_grad = call(
        last_kernel,
        v(own, up, down, up_far, down_far) + s(counts),
        [((1, n, units), F32), ((1, units, n), F32)],
    )
    sum_before, sum_after = call(
        pass_kernel, v(sum_before, sum_after, sum_low, sum_high), [((rows, 2 * feats), BF)] * 2
    )
    mixed, input_grad = call(
        rows_kernel, v(tokens, cotangent, sum_own, to_y(sum_after, 1), to_y(then(sum_before, (low, high)), -1)), [((1, rows, feats), BF)] * 2
    )
    return (mixed, input_grad, up_grad, down_grad)


def solution(mesh):
    in_specs = (
        P("dp", "block", None),
        P("dp", "block", None),
        P("block", None, None),
        P("block", None, None),
        P(),
        P(),
        P(),
    )
    out_specs = (
        P("dp", "block", None),
        P("dp", "block", None),
        P("block", "dp", None),
        P("block", None, "dp"),
    )
    return jax.shard_map(local, mesh=mesh, in_specs=in_specs, out_specs=out_specs, check_vma=False)
```
